512 devices in a mesh: section: 2 (over y_lo), channel: 16 (over x, y_hi), block: 16 (over z, core).
Axes of the slice: x: 4, y: 8 (y_hi: 4, y_lo: 2; y = y_hi * 2 + y_lo), z: 8, core: 2. Of those that a mesh axis runs over, the one named last changes fastest.
Arguments:
- env: bfloat16 [2, 16, 16, 512, 512], P('section', 'channel', 'block'), may hold values from -6 to 6
- site_tensor: bfloat16 [2, 4, 16, 512, 512], P('section', None, 'block'), may hold values from -0.25 to 0.25
- mpo: bfloat16 [2, 16, 16, 4], P('section'), may hold values from -2 to 2
- channel_mask: int32 [2, 16, 16], P('section'), may hold values 0 or 1
- block_mask: int32 [2, 4, 16], P('section', None, 'block'), may hold values 0 or 1
- state_charge: int32 [4], replicated, may hold values from 0 to 1, as said below
- psi: bfloat16 [2, 16, 512, 512], P('section', 'block'), may hold values from -0.0014648438 to 0.0014648438
Outputs:
- new_env: bfloat16 [2, 16, 16, 512, 512], P('section', 'channel', 'block')
- new_psi: bfloat16 [512, 2, 16, 512], P('channel', 'section', 'block')
The draws below stay inside these ranges and needn't reach their ends.
Inputs may be any that keep to these rules, and one draw needn't show every extreme that they name: `state_charge`: half of the 4 site states carry charge 0, the others charge 1.
All inputs are finite; a program needn't handle non-finite values. No bound on the sum of `channel_mask` or of `block_mask` on one device may be relied on, other than what follows from the above.
Results may differ from the reference program's by a relative error of at most 0.017.
Values may be sent and summed in bfloat16 or wider, within the bound.
A program may use at most 64 MiB of HBM per device.

```python
import jax
import jax.numpy as jnp
from jax import lax

SDIM = 512
SECTORS = 16
CHAN = 16
STATES = 4
VECS = 2


def draw_state_charge(key, part):
    base_charge = (jnp.arange(STATES) % 2).astype(jnp.int32)
    return jax.random.permutation(key, base_charge)


def with_ends(values, key, least, top_value):
    longest = values.shape.index(max(values.shape))
    spots = []
    for shift in (0, 1):
        where = [jax.random.randint(jax.random.fold_in(key, axis), (), 0, length) for axis, length in enumerate(values.shape)]
        where[longest] = (where[longest] + shift) % values.shape[longest]
        spots.append(tuple(where))
    return values.at[spots[0]].set(least).at[spots[1]].set(top_value)


def block_scale(own_key, shape, cuts, smallest, high):
    loudness, own = 1.0, jax.random.fold_in(own_key, 6)
    for dim, shards_of in cuts:
        draws = jnp.exp(jax.random.uniform(jax.random.fold_in(own, dim), (shards_of,), jnp.float32, smallest / len(cuts), high / len(cuts)))
        loudness = loudness * jnp.repeat(draws, shape[dim] // shards_of).reshape([-1 if axis == dim else 1 for axis in range(len(shape))])
    return loudness


def centred(stream_key, shape, spread, limit, pieces=(), dtype=jnp.bfloat16):
    entries = spread * jax.random.normal(stream_key, shape, jnp.float32)
    if pieces:
        entries = entries * block_scale(stream_key, shape, pieces, -0.22, 0.18)
    return jnp.clip(entries, -limit, limit).astype(dtype)


def setup_inputs(seed: int = 0) -> dict:
    key_list = jax.random.split(jax.random.key(seed), 8)
    env = centred(key_list[0], (2, CHAN, SECTORS, SDIM, SDIM), 1.0, 6.0, ((0, 2), (1, 16), (2, 16)))
    site_tensor = centred(key_list[1], (2, STATES, SECTORS, SDIM, SDIM), SDIM ** -0.5, 0.25, ((0, 2), (2, 16)))
    mpo = centred(key_list[2], (2, CHAN, CHAN, STATES), (CHAN // 2) ** -0.5, 2.0, ((0, 2),))
    channel_mask = with_ends((jax.random.randint(key_list[3], (2, CHAN, CHAN), 0, 2) < 1).astype(jnp.int32), jax.random.fold_in(key_list[3], 1), 0, 1)
    block_mask = with_ends((jax.random.randint(key_list[4], (2, STATES, SECTORS), 0, 4) < 3).astype(jnp.int32), jax.random.fold_in(key_list[4], 1), 0, 1)
    state_charge = draw_state_charge(jax.random.fold_in(key_list[7], 71), 0)
    psi = centred(key_list[6], (VECS, SECTORS, SDIM, SDIM), (0.125 / SDIM), 0.0014648438, ((0, 2), (1, 16)))
    return dict(env=env, site_tensor=site_tensor, mpo=mpo, channel_mask=channel_mask, block_mask=block_mask, state_charge=state_charge, psi=psi)


def sector_env(weights, charge_label, env_q, site_q, mask_q):
    blended_environment = jnp.einsum("wvs,wab->vsab", weights, env_q.astype(jnp.float32)).astype(jnp.bfloat16)
    product = jnp.einsum("vsac,scb->vsab", blended_environment.astype(jnp.float32), site_q.astype(jnp.float32)).astype(jnp.bfloat16)
    contracted_layers = jnp.einsum("sca,vscb->vsab", site_q.astype(jnp.float32), product.astype(jnp.float32))
    sector_present = mask_q.astype(jnp.float32)
    resident_part = jnp.einsum("dixh,i->dxh", contracted_layers, sector_present * (1.0 - charge_label))
    outgoing_part = jnp.einsum("dixh,i->dxh", contracted_layers, sector_present * charge_label).astype(jnp.bfloat16)
    return resident_part, outgoing_part


def sector_psi(left_q, right_q, psi_q):
    applied = jnp.einsum("wab,vbd->wvad", left_q.astype(jnp.float32), psi_q.astype(jnp.float32)).astype(jnp.bfloat16)
    return jnp.einsum("wvad,wcd->avc", applied.astype(jnp.float32), right_q.astype(jnp.float32))


def reference(env, site_tensor, mpo, channel_mask, block_mask, state_charge, psi):
    charge_label = state_charge.astype(jnp.float32)
    results = []
    for section_index in range(2):
        weights = mpo[section_index].astype(jnp.float32) * channel_mask[section_index].astype(jnp.float32)[:, :, None]

        def per_sector(inputs):
            return sector_env(weights, charge_label, inputs[0], inputs[1], inputs[2])

        resident_part, outgoing_part = lax.map(per_sector, (jnp.moveaxis(env[section_index], 1, 0), jnp.moveaxis(site_tensor[section_index], 1, 0), block_mask[section_index].T))
        empty = jnp.zeros_like(outgoing_part[:1])
        if section_index == 0:
            shifted = jnp.concatenate([empty, outgoing_part[:-1]], axis=0)
        else:
            shifted = jnp.concatenate([outgoing_part[1:], empty], axis=0)
        advanced = (resident_part + shifted.astype(jnp.float32)).astype(jnp.bfloat16)
        results.append(jnp.moveaxis(advanced, 0, 1))
    new_env = jnp.stack(results, axis=0)

    def per_block(inputs):
        return sector_psi(inputs[0], inputs[1], inputs[2])

    applied = lax.map(per_block, (jnp.moveaxis(new_env[0], 1, 0), jnp.moveaxis(new_env[1], 1, 0), jnp.moveaxis(psi, 1, 0)))
    new_psi = jnp.transpose(applied, (1, 2, 0, 3)).astype(jnp.bfloat16)
    return new_env, new_psi
```

```python
import functools

import jax
import jax.numpy as jnp
from jax import lax
from jax.experimental import pallas as pl
from jax.experimental.pallas import tpu as pltpu
from jax.sharding import PartitionSpec as P

MESH = pl.DeviceIdType.MESH
F32, BF16 = jnp.float32, jnp.bfloat16
N = 512
NX = 4
NY = 4
NCH = 4
R = 128 // NCH
SUB = R // 16
LAST = (((1,), (1,)), ((), ()))


def mod4(value):
    return lax.rem(value, 4)


def mix_matrix(mpo_ref, cmask_ref, bmask_ref, charge_ref, yh):
    rows = lax.broadcasted_iota(jnp.int32, (256, 16), 0)
    lane = lax.broadcasted_iota(jnp.int32, (256, 16), 1)
    want_v = lax.rem(rows // 16, 4) * 4 + yh
    pick_v = (lane == want_v).astype(F32)
    rows_s = lax.broadcasted_iota(jnp.int32, (256, 4), 0)
    lane_s = lax.broadcasted_iota(jnp.int32, (256, 4), 1)
    slots, _ = state_slots(charge_ref)
    pick_s = jnp.zeros((256, 4), F32)
    for s in range(4):
        hit = (lane_s == s) & (rows_s // 64 == slots[s])
        pick_s = jnp.where(hit, bmask_ref[s].astype(F32), pick_s)
    pick_s = pick_s.astype(BF16)
    cmask = cmask_ref[...].astype(F32).astype(BF16)
    allowed = lax.dot_general(pick_v.astype(BF16), cmask, LAST, preferred_element_type=F32)
    values = jnp.zeros((256, 16), F32)
    for w in range(16):
        coupling = jnp.dot(pick_s, mpo_ref[w], preferred_element_type=F32) * pick_v
        column = jnp.sum(coupling, axis=1, keepdims=True)
        values = jnp.where(lane == w, column, values)
    values = values * allowed
    spread_w = lax.broadcasted_iota(jnp.int32, (16, 256), 0)
    spread_c = lax.broadcasted_iota(jnp.int32, (16, 256), 1) // 16
    spread = (spread_w == lax.rem(spread_c, 4) * 4 + spread_c // 4).astype(BF16)
    full = jnp.dot(values.astype(BF16), spread, preferred_element_type=F32)
    row = lax.broadcasted_iota(jnp.int32, (256, 256), 0)
    col = lax.broadcasted_iota(jnp.int32, (256, 256), 1)
    return jnp.where(lax.rem(row, 16) == lax.rem(col, 16), full, 0.0).astype(BF16)


def state_slots(charge_ref):
    charge = [charge_ref[s] for s in range(4)]
    slots = []
    ones = jnp.int32(0)
    for s in range(4):
        slots.append(jnp.where(charge[s] == 1, 2 + ones, s - ones))
        ones = ones + charge[s]
    order = []
    for k in range(4):
        place = jnp.int32(0)
        for s in range(4):
            place = place + jnp.where(slots[s] == k, s, 0)
        order.append(place)
    return slots, order


def kernel(
    charge_ref, bmask_ref, env_ref, site_ref, mpo_ref, cmask_ref, psi_ref,
    new_env_ref, new_psi_ref,
    site_v, srt, near, psi_v, psi_t, kmat, gath, mixed, sent, prod, turned, acc,
    mine, other, half, zsum, zparts, zrows, ysend, yrecv,
    site_sem, psi_sem, own_sem, out_sem,
    x_send, x_recv, y_send, y_recv, r_send, r_recv, near_send, near_recv,
    p_send, p_recv, n_send, n_recv, z_send, z_recv, f_send, f_recv,
):
    g = lax.axis_index("section")
    c = lax.axis_index("channel")
    q = lax.axis_index("block")
    x, yh = c // 4, lax.rem(c, 4)
    up = lax.rem(q + 1, 16)
    down = lax.rem(q + 15, 16)
    target = jnp.where(g == 0, up, down)
    origin = jnp.where(g == 0, down, up)
    fed = jnp.where(g == 0, q > 0, q < 15)
    at_x = [mod4(x + i) * 4 + yh for i in range(4)]
    at_y = [x * 4 + mod4(yh + i) for i in range(4)]

    def to(channel=None, block=None, section=None):
        where = {}
        if section is not None:
            where["section"] = section
        if channel is not None:
            where["channel"] = channel
        if block is not None:
            where["block"] = block
        return where

    def send(src, dst, send_sem, recv_sem, where):
        pltpu.make_async_remote_copy(
            src_ref=src, dst_ref=dst, send_sem=send_sem, recv_sem=recv_sem, device_id=where, device_id_type=MESH
        ).start()

    def took(ref, sem):
        pltpu.make_async_copy(ref, ref, sem).wait()

    site_in = pltpu.make_async_copy(site_ref, site_v, site_sem)
    site_in.start()
    psi_in = pltpu.make_async_copy(psi_ref, psi_v, psi_sem)
    psi_in.start()
    for j in range(NCH):
        pltpu.make_async_copy(env_ref.at[pl.ds(x * 128 + j * R, R)], gath.at[j, yh * 4 + x], own_sem).start()

    barrier = pltpu.get_barrier_semaphore()
    for i in range(1, 4):
        pl.semaphore_signal(barrier, inc=1, device_id=to(channel=at_x[i]), device_id_type=MESH)
        pl.semaphore_signal(barrier, inc=1, device_id=to(channel=at_y[i]), device_id_type=MESH)
    for i in range(4):
        pl.semaphore_signal(barrier, inc=1, device_id=to(channel=at_x[i], block=origin), device_id_type=MESH)
    pl.semaphore_signal(barrier, inc=1, device_id=to(section=1 - g), device_id_type=MESH)
    pl.semaphore_wait(barrier, 11)

    for j in range(NCH):
        for i in range(1, 4):
            send(
                env_ref.at[pl.ds(mod4(x + i) * 128 + j * R, R)], gath.at[j, yh * 4 + x],
                x_send, x_recv.at[j], to(channel=at_x[i]),
            )

    site_in.wait()
    _, order = state_slots(charge_ref)
    for k in range(4):
        srt[k] = site_v[order[k]]
    send(srt.at[pl.ds(2, 2)], near, near_send, near_recv, to(block=target))

    def pass_on(j):
        took(gath.at[j, pl.ds(0, 3)], x_recv.at[j])
        rows = gath.at[j, pl.ds(yh * 4, 4)]
        send(rows, rows, y_send, y_recv.at[j, 0], to(channel=at_y[1]))
        send(rows, rows, y_send, y_recv.at[j, 1], to(channel=at_y[3]))

    def relay(j):
        before = gath.at[j, pl.ds(mod4(yh + 3) * 4, 2)]
        took(gath.at[j, pl.ds(0, 4)], y_recv.at[j, 0])
        send(before, before, r_send, r_recv.at[j, 0], to(channel=at_y[1]))
        after = gath.at[j, pl.ds(mod4(yh + 1) * 4 + 2, 2)]
        took(gath.at[j, pl.ds(0, 4)], y_recv.at[j, 1])
        send(after, after, r_send, r_recv.at[j, 1], to(channel=at_y[3]))

    def multiply(j):
        took(gath.at[j, pl.ds(0, 2)], r_recv.at[j, 0])
        took(gath.at[j, pl.ds(0, 2)], r_recv.at[j, 1])
        for sub in range(SUB):
            piece = gath[j, :, sub * 16 : sub * 16 + 16, :].reshape(256, N)
            blended = jnp.dot(kmat[...], piece, preferred_element_type=F32)
            mixed[:, sub * 16 : sub * 16 + 16, :] = blended.astype(BF16).reshape(16, 16, N)
        for k in range(4):
            product = jnp.dot(mixed[4 * k : 4 * k + 4].reshape(4 * R, N), srt[k], preferred_element_type=F32)
            product = product.astype(BF16).reshape(4, R, N)
            for vx in range(4):
                sent[j, vx * 4 + k] = product[vx]
        for i in range(1, 4):
            v = mod4(x + i)
            send(sent.at[j, pl.ds(v * 4, 2)], prod.at[j, pl.ds(x * 4, 2)], p_send, p_recv.at[j], to(channel=at_x[i]))
        for i in range(4):
            v = mod4(x + i)
            send(
                sent.at[j, pl.ds(v * 4 + 2, 2)], prod.at[j, pl.ds(x * 4 + 2, 2)],
                p_send, p_recv.at[j], to(channel=at_x[i], block=target),
            )
        prod[j, pl.ds(x * 4, 2)] = sent[j, pl.ds(x * 4, 2)]

    def accumulate(j):
        took(prod.at[j, pl.ds(0, 14)], p_recv.at[j])

        def tile(t, carry):
            rows = pl.ds(pl.multiple_of(t * 128, 128), 128)
            part = jnp.dot(turned[j, rows, :], prod[j].reshape(16 * R, N), preferred_element_type=F32)
            acc[rows, :] = part if j == 0 else acc[rows, :] + part
            return carry

        lax.fori_loop(0, 4, tile, 0)

    def turn(k):
        for j in range(NCH):
            for xs in range(4):
                rows = slice(xs * 128 + j * R, xs * 128 + j * R + R)
                block = srt[k, rows, :] if k < 2 else jnp.where(fed, near[k - 2, rows, :].astype(F32), 0.0).astype(BF16)
                columns = slice((xs * 4 + k) * R, (xs * 4 + k) * R + R)
                turned[j, :, columns] = block.T

    took(gath.at[0:NCH, 0], own_sem)
    pass_on(0)
    pass_on(1)

    kmat[...] = mix_matrix(mpo_ref, cmask_ref, bmask_ref, charge_ref, yh)
    psi_in.wait()

    @pl.when(g == 0)
    def _():
        psi_t[...] = psi_v[...]

    @pl.when(g == 1)
    def _():
        psi_t[...] = psi_v[...].T

    turn(0)
    turn(1)

    for j in range(NCH):
        relay(j)
        if j + 2 < NCH:
            pass_on(j + 2)
        if j == 0:
            took(near, near_recv)
            turn(2)
            turn(3)
        if j >= 1:
            multiply(j - 1)
        if j >= 2:
            accumulate(j - 2)
    multiply(NCH - 1)
    accumulate(NCH - 2)

    final = NCH - 1
    took(prod.at[final, pl.ds(0, 14)], p_recv.at[final])
    starts = [pl.multiple_of(mod4(x + i) * 128, 128) for i in range(4)]
    for i in (1, 2, 3, 0):
        rows = pl.ds(starts[i], 128)
        part = jnp.dot(turned[final, rows, :], prod[final].reshape(16 * R, N), preferred_element_type=F32)
        mine[rows, :] = (acc[rows, :] + part).astype(BF16)
        send(mine.at[rows], other.at[rows], n_send, n_recv.at[i], to(section=1 - g))
    out = pltpu.make_async_copy(mine, new_env_ref, out_sem)
    out.start()
    for i in range(4):
        rows = pl.ds(i * 128, 128)
        half[rows, :] = jnp.dot(mine[rows, :], psi_t[...], preferred_element_type=F32).astype(BF16)

    @pl.when(g == 0)
    def _():
        for i in (1, 2, 3, 0):
            rows = pl.ds(starts[i], 128)
            took(other.at[pl.ds(0, 128)], n_recv.at[i])
            part = lax.dot_general(half[...], other[rows, :], LAST, preferred_element_type=F32)
            zsum[:, rows] = part.astype(BF16)
            for d in range(1, 4):
                send(
                    zsum.at[pl.ds(starts[d], 128), rows], zparts.at[x, :, rows],
                    z_send, z_recv, to(channel=at_x[d]),
                )

    @pl.when(g == 1)
    def _():
        for d in (1, 2, 3, 0):
            rows = pl.ds(starts[d], 128)
            took(other.at[pl.ds(0, 128)], n_recv.at[d])
            part = lax.dot_general(other[rows, :], half[...], LAST, preferred_element_type=F32)
            zsum[rows, :] = part.astype(BF16)
            if d:
                send(zsum.at[rows], zparts.at[x], z_send, z_recv, to(channel=at_x[d]))

    took(zparts.at[pl.ds(0, 3)], z_recv)
    total = zsum[pl.ds(starts[0], 128), :].astype(F32)
    for d in range(1, 4):
        total = total + zparts[mod4(x + d)].astype(F32)
    zrows[...] = total
    ysend[...] = total.astype(BF16).reshape(4, 32, N)
    for d in range(1, 4):
        send(ysend.at[mod4(yh + d)], yrecv.at[yh], f_send, f_recv, to(channel=at_y[d]))
    took(yrecv.at[pl.ds(0, 3)], f_recv)
    result = zrows[pl.ds(pl.multiple_of(yh * 32, 32), 32), :]
    for d in range(1, 4):
        result = result + yrecv[mod4(yh + d)].astype(F32)
    new_psi_ref[...] = result.astype(BF16)

    out.wait()
    took(gath.at[0 : NCH, 0 : 3], x_send)
    took(gath.at[0 : NCH, 0 : 8], y_send)
    took(gath.at[0 : NCH, 0 : 4], r_send)
    took(near, near_send)
    took(sent.at[0 : NCH, 0 : 14], p_send)
    took(mine, n_send)
    took(zparts.at[pl.ds(0, 3)], z_send)
    took(ysend.at[pl.ds(0, 3)], f_send)


def per_device(env, site_tensor, mpo, channel_mask, block_mask, state_charge, psi):
    dma = pltpu.SemaphoreType.DMA
    hbm = pl.BlockSpec(memory_space=pl.ANY)
    vmem = pl.BlockSpec(memory_space=pltpu.VMEM)
    smem = pl.BlockSpec(memory_space=pltpu.SMEM)
    new_env, new_psi = pl.pallas_call(
        kernel,
        out_shape=(jax.ShapeDtypeStruct((N, N), BF16), jax.ShapeDtypeStruct((32, N), BF16)),
        in_specs=[smem, smem, hbm, hbm, vmem, vmem, hbm],
        out_specs=(hbm, vmem),
        scratch_shapes=[
            pltpu.VMEM((4, N, N), BF16),
            pltpu.VMEM((4, N, N), BF16),
            pltpu.VMEM((2, N, N), BF16),
            pltpu.VMEM((N, N), BF16),
            pltpu.VMEM((N, N), BF16),
            pltpu.VMEM((256, 256), BF16),
            pltpu.VMEM((NCH, 16, R, N), BF16),
            pltpu.VMEM((16, R, N), BF16),
            pltpu.VMEM((NCH, 16, R, N), BF16),
            pltpu.VMEM((NCH, 16, R, N), BF16),
            pltpu.VMEM((NCH, N, 16 * R), BF16),
            pltpu.VMEM((N, N), F32),
            pltpu.VMEM((N, N), BF16),
            pltpu.VMEM((N, N), BF16),
            pltpu.VMEM((N, N), BF16),
            pltpu.VMEM((N, N), BF16),
            pltpu.VMEM((4, 128, N), BF16),
            pltpu.VMEM((128, N), F32),
            pltpu.VMEM((4, 32, N), BF16),
            pltpu.VMEM((4, 32, N), BF16),
            dma, dma, dma, dma,
            dma, dma((NCH,)), dma, dma((NCH, 2)), dma, dma((NCH, 2)), dma, dma,
            dma, dma((NCH,)), dma, dma((4,)), dma, dma, dma, dma,
        ],
        compiler_params=pltpu.CompilerParams(
            collective_id=0, has_side_effects=True, vmem_limit_bytes=40 * 1024 * 1024
        ),
    )(
        state_charge,
        block_mask.reshape(4),
        env.reshape(N, N),
        site_tensor.reshape(4, N, N),
        jnp.swapaxes(mpo[0], 1, 2),
        channel_mask[0],
        psi.reshape(N, N),
    )
    return new_env.reshape(1, 1, 1, N, N), new_psi.reshape(32, 1, 1, N)


def solution(mesh):
    return jax.shard_map(
        per_device,
        mesh=mesh,
        in_specs=(
            P("section", "channel", "block", None, None),
            P("section", None, "block", None, None),
            P("section", None, None, None),
            P("section", None, None),
            P("section", None, "block"),
            P(),
            P("section", "block", None, None),
        ),
        out_specs=(
            P("section", "channel", "block", None, None),
            P("channel", "section", "block", None),
        ),
        check_vma=False,
    )
```

```python
import functools

import jax
import jax.numpy as jnp
from jax import lax
from jax.experimental import pallas as pl
from jax.experimental.pallas import tpu as pltpu
from jax.sharding import PartitionSpec as P

MESH = pl.DeviceIdType.MESH
F32, BF16 = jnp.float32, jnp.bfloat16
N = 512
BLOCKS = 8
CHUNKS = ((0, 1), (1, 1), (2, 1), (3, 1), (4, 1), (5, 1), (6, 1), (7, 1))
SWAPS = ((0, 1), (1, 1), (2, 6))
NCH = len(CHUNKS)
WIDEST = max(n for _, n in CHUNKS)
LAG = 4
LAST = (((1,), (1,)), ((), ()))


def mod4(value):
    return lax.rem(value, 4)


def mix_matrix(mpo_ref, cmask_ref, bmask_ref, charge_ref, yh):
    rows = lax.broadcasted_iota(jnp.int32, (256, 16), 0)
    lane = lax.broadcasted_iota(jnp.int32, (256, 16), 1)
    want_v = lax.rem(rows // 16, 4) * 4 + yh
    pick_v = (lane == want_v).astype(F32)
    rows_s = lax.broadcasted_iota(jnp.int32, (256, 4), 0)
    lane_s = lax.broadcasted_iota(jnp.int32, (256, 4), 1)
    slots, _ = state_slots(charge_ref)
    pick_s = jnp.zeros((256, 4), F32)
    for s in range(4):
        hit = (lane_s == s) & (rows_s // 64 == slots[s])
        pick_s = jnp.where(hit, bmask_ref[s].astype(F32), pick_s)
    pick_s = pick_s.astype(BF16)
    cmask = cmask_ref[...].astype(F32).astype(BF16)
    allowed = lax.dot_general(pick_v.astype(BF16), cmask, LAST, preferred_element_type=F32)
    values = jnp.zeros((256, 16), F32)
    for w in range(16):
        coupling = jnp.dot(pick_s, mpo_ref[w], preferred_element_type=F32) * pick_v
        column = jnp.sum(coupling, axis=1, keepdims=True)
        values = jnp.where(lane == w, column, values)
    values = values * allowed
    spread_w = lax.broadcasted_iota(jnp.int32, (16, 256), 0)
    spread_c = lax.broadcasted_iota(jnp.int32, (16, 256), 1) // 16
    spread = (spread_w == lax.rem(spread_c, 4) * 4 + spread_c // 4).astype(BF16)
    full = jnp.dot(values.astype(BF16), spread, preferred_element_type=F32)
    row = lax.broadcasted_iota(jnp.int32, (256, 256), 0)
    col = lax.broadcasted_iota(jnp.int32, (256, 256), 1)
    return jnp.where(lax.rem(row, 16) == lax.rem(col, 16), full, 0.0).astype(BF16)


def state_slots(charge_ref):
    charge = [charge_ref[s] for s in range(4)]
    slots = []
    ones = jnp.int32(0)
    for s in range(4):
        slots.append(jnp.where(charge[s] == 1, 2 + ones, s - ones))
        ones = ones + charge[s]
    order = []
    for k in range(4):
        place = jnp.int32(0)
        for s in range(4):
            place = place + jnp.where(slots[s] == k, s, 0)
        order.append(place)
    return slots, order


def kernel(
    charge_in, bmask_in, env_ref, site_ref, mpo_in, cmask_in, psi_ref,
    new_env_ref, new_psi_ref,
    charge_ref, bmask_ref, mpo_ref, cmask_ref,
    site_v, srt, near, psi_v, psi_t, kmat, gath, mixed, sent, prod, turned, acc,
    other, half, wide, wide_in, summed, kept, ysend, yrecv,
    small_sem, site_sem, psi_sem, own_sem,
    x_send, x_recv, y_send, y_recv, w_recv, r_send, r_recv, near_send, near_recv,
    p_send, p_recv, n_send, n_recv, z_send, z_recv, f_send, f_recv,
):
    g = lax.axis_index("section")
    c = lax.axis_index("channel")
    q = lax.axis_index("block")
    x, yh = c // 4, lax.rem(c, 4)
    up = lax.rem(q + 1, 16)
    down = lax.rem(q + 15, 16)
    target = jnp.where(g == 0, up, down)
    origin = jnp.where(g == 0, down, up)
    fed = jnp.where(g == 0, q > 0, q < 15)
    at_x = [mod4(x + i) * 4 + yh for i in range(4)]
    at_y = [x * 4 + mod4(yh + i) for i in range(4)]
    spans = [pl.ds(first, count) for first, count in CHUNKS]

    def to(channel=None, block=None, section=None):
        where = {}
        if section is not None:
            where["section"] = section
        if channel is not None:
            where["channel"] = channel
        if block is not None:
            where["block"] = block
        return where

    def send(src, dst, send_sem, recv_sem, where):
        pltpu.make_async_remote_copy(
            src_ref=src, dst_ref=dst, send_sem=send_sem, recv_sem=recv_sem, device_id=where, device_id_type=MESH
        ).start()

    def took(ref, sem):
        pltpu.make_async_copy(ref, ref, sem).wait()

    small = [
        pltpu.make_async_copy(charge_in, charge_ref, small_sem.at[0]),
        pltpu.make_async_copy(bmask_in, bmask_ref, small_sem.at[1]),
        pltpu.make_async_copy(mpo_in, mpo_ref, small_sem.at[2]),
        pltpu.make_async_copy(cmask_in, cmask_ref, small_sem.at[3]),
    ]
    for copy in small:
        copy.start()
    own_in = pltpu.make_async_copy(env_ref.at[pl.ds(x * BLOCKS, BLOCKS)], gath.at[:, yh * 4 + x], own_sem)
    own_in.start()
    site_in = pltpu.make_async_copy(site_ref, site_v, site_sem)
    site_in.start()
    psi_in = pltpu.make_async_copy(psi_ref, psi_v, psi_sem)
    psi_in.start()

    barrier = pltpu.get_barrier_semaphore()
    for i in range(1, 4):
        pl.semaphore_signal(barrier, inc=1, device_id=to(channel=at_x[i]), device_id_type=MESH)
        pl.semaphore_signal(barrier, inc=1, device_id=to(channel=at_y[i]), device_id_type=MESH)
    for i in range(4):
        pl.semaphore_signal(barrier, inc=1, device_id=to(channel=at_x[i], block=origin), device_id_type=MESH)
    pl.semaphore_signal(barrier, inc=1, device_id=to(section=1 - g), device_id_type=MESH)
    pl.semaphore_wait(barrier, 11)

    for j, (first, count) in enumerate(SWAPS):
        for i in range(1, 4):
            send(
                env_ref.at[pl.ds(mod4(x + i) * BLOCKS + first, count)], gath.at[pl.ds(first, count), yh * 4 + x],
                x_send, x_recv.at[j], to(channel=at_x[i]),
            )

    def pass_on(j):
        if j < len(SWAPS):
            took(gath.at[pl.ds(*SWAPS[j]), pl.ds(0, 3)], x_recv.at[j])
        early = gath.at[spans[j], pl.ds(yh * 4, 2)]
        late = gath.at[spans[j], pl.ds(yh * 4 + 2, 2)]
        send(early, early, y_send, y_recv.at[j, 0], to(channel=at_y[1]))
        send(late, late, y_send, y_recv.at[j, 1], to(channel=at_y[3]))
        send(late, late, y_send, w_recv.at[j, 0], to(channel=at_y[1]))
        send(early, early, y_send, w_recv.at[j, 1], to(channel=at_y[3]))

    def relay(j):
        two = gath.at[spans[j], pl.ds(0, 2)]
        before = gath.at[spans[j], pl.ds(mod4(yh + 3) * 4, 2)]
        took(two, y_recv.at[j, 0])
        send(before, before, r_send, r_recv.at[j, 0], to(channel=at_y[1]))
        after = gath.at[spans[j], pl.ds(mod4(yh + 1) * 4 + 2, 2)]
        took(two, y_recv.at[j, 1])
        send(after, after, r_send, r_recv.at[j, 1], to(channel=at_y[3]))

    def multiply(j):
        first, count = CHUNKS[j]
        for way in range(2):
            took(gath.at[spans[j], pl.ds(0, 2)], w_recv.at[j, way])
            took(gath.at[spans[j], pl.ds(0, 2)], r_recv.at[j, way])
        for i in range(count):
            blended = jnp.dot(kmat[...], gath[first + i].reshape(256, N), preferred_element_type=F32)
            mixed[:, i] = blended.astype(BF16).reshape(4, 4, 16, N)
        for k in range(4):
            product = jnp.dot(mixed[k, 0:count].reshape(count * 64, N), srt[k], preferred_element_type=F32)
            product = product.astype(BF16).reshape(count, 4, 16, N)
            for vx in range(4):
                sent[first : first + count, vx * 4 + k] = product[:, vx]
        for i in range(1, 4):
            v = mod4(x + i)
            send(
                sent.at[spans[j], pl.ds(v * 4, 2)], prod.at[spans[j], pl.ds(x * 4, 2)],
                p_send, p_recv.at[j], to(channel=at_x[i]),
            )
        for i in range(4):
            v = mod4(x + i)
            send(
                sent.at[spans[j], pl.ds(v * 4 + 2, 2)], prod.at[spans[j], pl.ds(x * 4 + 2, 2)],
                p_send, p_recv.at[j], to(channel=at_x[i], block=target),
            )
        prod[first : first + count, pl.ds(x * 4, 2)] = sent[first : first + count, pl.ds(x * 4, 2)]

    def turn(j):
        first, count = CHUNKS[j]
        for b in range(first, first + count):
            pieces = []
            for xs in range(4):
                rows = slice(xs * 128 + b * 16, xs * 128 + b * 16 + 16)
                pieces += [srt[0, rows, :], srt[1, rows, :], near[0, rows, :], near[1, rows, :]]
            turned[b] = jnp.concatenate(pieces, axis=0).T.reshape(4, 4, 32, 256)

    def gained(j, tile):
        first, count = CHUNKS[j]
        part = jnp.zeros((128, N), F32)
        for b in range(first, first + count):
            left = turned[(b, *tile)].reshape(128, 256)
            part = part + jnp.dot(left, prod[b].reshape(256, N), preferred_element_type=F32)
        return part.reshape(4, 32, N)

    def accumulate(j):
        took(prod.at[spans[j], pl.ds(0, 14)], p_recv.at[j])

        def add(t, carry):
            part = gained(j, (t,))
            acc[t] = part if j == 0 else acc[t] + part
            return carry

        lax.fori_loop(0, 4, add, 0)

    def advance(tile, recv_sem):
        new_env_ref[tile] = (acc[tile] + gained(NCH - 1, tile)).astype(BF16)
        send(new_env_ref.at[tile], other.at[tile], n_send, recv_sem, to(section=1 - g))

    for copy in small:
        copy.wait()
    own_in.wait()
    pass_on(0)
    site_in.wait()
    _, order = state_slots(charge_ref)
    for k in (2, 3, 0, 1):
        srt[k] = site_v[order[k]]
        if k == 3:
            send(srt.at[pl.ds(2, 2)], near, near_send, near_recv, to(block=target))
    pass_on(1)
    kmat[...] = mix_matrix(mpo_ref, cmask_ref, bmask_ref, charge_ref, yh)

    for j in range(NCH):
        relay(j)
        if j + 2 < NCH:
            pass_on(j + 2)
        if j == 1:
            psi_in.wait()

            @pl.when(g == 0)
            def _():
                psi_t[...] = psi_v[...]

            @pl.when(g == 1)
            def _():
                psi_t[...] = psi_v[...].T

        if j == LAG - 1:
            took(near, near_recv)

            @pl.when(jnp.logical_not(fed))
            def _():
                near[...] = jnp.zeros_like(near)

        if j >= LAG:
            accumulate(j - LAG)
        if j >= 1:
            multiply(j - 1)
        if j >= LAG - 1:
            turn(j - LAG + 1)
    multiply(NCH - 1)
    for j in range(NCH - LAG + 1, NCH):
        turn(j)
    for j in range(NCH - LAG, NCH - 1):
        accumulate(j)

    took(prod.at[spans[-1], pl.ds(0, 14)], p_recv.at[NCH - 1])
    all_rows = slice(None)
    hand = [mod4(yh + d) for d in range(4)]

    @pl.when(g == 0)
    def _():
        for d in (1, 2, 3, 0):
            advance((all_rows, hand[d]), n_recv.at[d])

    @pl.when(g == 1)
    def _():
        for t in range(4):
            advance((t,), n_recv.at[t])

    for t in range(4):
        rows = new_env_ref[t].reshape(128, N)
        half[t] = jnp.dot(rows, psi_t[...], preferred_element_type=F32).astype(BF16).reshape(4, 32, N)
    quarter = other.at[0]

    @pl.when(g == 0)
    def _():
        def settle(t):
            columns = slice(t * 128, t * 128 + 128)
            took(wide_in.at[pl.ds(0, 3), :, :, columns], z_recv.at[t])
            total = wide[x, :, :, columns].astype(F32)
            for d in range(1, 4):
                total = total + wide_in[mod4(x + d), :, :, columns].astype(F32)
            summed[:, :, columns] = total
            ysend[:, :, columns] = total.astype(BF16)
            for d in range(1, 4):
                send(
                    ysend.at[hand[d], :, columns], yrecv.at[yh, :, columns],
                    f_send, f_recv, to(channel=at_y[d]),
                )

        for t in range(4):
            columns = slice(t * 128, t * 128 + 128)
            took(quarter, n_recv.at[t])
            part = lax.dot_general(half[...].reshape(N, N), other[t].reshape(128, N), LAST, preferred_element_type=F32)
            wide[:, :, :, columns] = part.astype(BF16).reshape(4, 4, 32, 128)
            for d in range(1, 4):
                send(
                    wide.at[mod4(x + d), :, :, columns], wide_in.at[x, :, :, columns],
                    z_send, z_recv.at[t], to(channel=at_x[d]),
                )
            if t:
                settle(t - 1)
        settle(3)
        kept[...] = summed[yh]

    @pl.when(g == 1)
    def _():
        def settle(d):
            took(wide_in.at[d, pl.ds(0, 3)], z_recv.at[d])
            total = wide[d, x].astype(F32)
            for e in range(1, 4):
                total = total + wide_in[d, mod4(x + e)].astype(F32)
            if d:
                ysend[d] = total.astype(BF16)
                send(ysend.at[d], yrecv.at[yh], f_send, f_recv, to(channel=at_y[d]))
            else:
                kept[...] = total

        for d in (1, 2, 3, 0):
            took(quarter, n_recv.at[d])
            rows = other[:, hand[d]].reshape(128, N)
            part = lax.dot_general(rows, half[...].reshape(N, N), LAST, preferred_element_type=F32)
            wide[d] = part.astype(BF16).reshape(4, 32, N)
            for e in range(1, 4):
                send(wide.at[d, mod4(x + e)], wide_in.at[d, x], z_send, z_recv.at[d], to(channel=at_x[e]))
            if d != 1:
                settle((d + 3) % 4)
        settle(0)

    took(gath.at[:, 0:3], x_send)
    took(gath.at[:, 0:8], y_send)
    took(gath.at[:, 0:4], r_send)
    took(near, near_send)
    took(sent.at[:, 0:14], p_send)
    took(new_env_ref, n_send)
    took(wide_in.at[pl.ds(0, 3)], z_send)
    took(yrecv.at[pl.ds(0, 3)], f_recv)
    result = kept[...]
    for d in range(1, 4):
        result = result + yrecv[mod4(yh + d)].astype(F32)
    new_psi_ref[...] = result.astype(BF16)
    took(ysend.at[pl.ds(0, 3)], f_send)


def per_device(env, site_tensor, mpo, channel_mask, block_mask, state_charge, psi):
    dma = pltpu.SemaphoreType.DMA
    hbm = pl.BlockSpec(memory_space=pltpu.HBM)
    vmem = pl.BlockSpec(memory_space=pltpu.VMEM)
    new_env, new_psi = pl.pallas_call(
        kernel,
        out_shape=(pltpu.VMEM((4, 4, 32, N), BF16), pltpu.VMEM((32, N), BF16)),
        in_specs=[hbm] * 7,
        out_specs=(vmem, vmem),
        scratch_shapes=[
            pltpu.SMEM((4,), jnp.int32),
            pltpu.SMEM((4,), jnp.int32),
            pltpu.VMEM((16, 4, 16), BF16),
            pltpu.VMEM((16, 16), jnp.int32),
            pltpu.VMEM((4, N, N), BF16),
            pltpu.VMEM((4, N, N), BF16),
            pltpu.VMEM((2, N, N), BF16),
            pltpu.VMEM((N, N), BF16),
            pltpu.VMEM((N, N), BF16),
            pltpu.VMEM((256, 256), BF16),
            pltpu.VMEM((BLOCKS, 16, 16, N), BF16),
            pltpu.VMEM((4, WIDEST, 4, 16, N), BF16),
            pltpu.VMEM((BLOCKS, 16, 16, N), BF16),
            pltpu.VMEM((BLOCKS, 16, 16, N), BF16),
            pltpu.VMEM((BLOCKS, 4, 4, 32, 256), BF16),
            pltpu.VMEM((4, 4, 32, N), F32),
            pltpu.VMEM((4, 4, 32, N), BF16),
            pltpu.VMEM((4, 4, 32, N), BF16),
            pltpu.VMEM((4, 4, 32, N), BF16),
            pltpu.VMEM((4, 4, 32, N), BF16),
            pltpu.VMEM((4, 32, N), F32),
            pltpu.VMEM((32, N), F32),
            pltpu.VMEM((4, 32, N), BF16),
            pltpu.VMEM((4, 32, N), BF16),
            dma((4,)), dma, dma, dma,
            dma, dma((len(SWAPS),)), dma, dma((NCH, 2)), dma((NCH, 2)), dma, dma((NCH, 2)), dma, dma,
            dma, dma((NCH,)), dma, dma((4,)), dma, dma((4,)), dma, dma,
        ],
        compiler_params=pltpu.CompilerParams(
            collective_id=0, has_side_effects=True, vmem_limit_bytes=56 * 1024 * 1024
        ),
    )(
        *[
            pltpu.with_memory_space_constraint(a, pltpu.HBM)
            for a in (
                state_charge,
                block_mask.reshape(4),
                env.reshape(4 * BLOCKS, 16, N),
                site_tensor.reshape(4, N, N),
                jnp.swapaxes(mpo[0], 1, 2),
                channel_mask[0],
                psi.reshape(N, N),
            )
        ]
    )
    return new_env.reshape(1, 1, 1, N, N), new_psi.reshape(32, 1, 1, N)


def solution(mesh):
    return jax.shard_map(
        per_device,
        mesh=mesh,
        in_specs=(
            P("section", "channel", "block", None, None),
            P("section", None, "block", None, None),
            P("section", None, None, None),
            P("section", None, None),
            P("section", None, "block"),
            P(),
            P("section", "block", None, None),
        ),
        out_specs=(
            P("section", "channel", "block", None, None),
            P("channel", "section", "block", None),
        ),
        check_vma=False,
    )
```

```python
import functools

import jax
import jax.numpy as jnp
from jax import lax
from jax.experimental import pallas as pl
from jax.experimental.pallas import tpu as pltpu
from jax.sharding import PartitionSpec as P

MESH = pl.DeviceIdType.MESH
F32, BF16 = jnp.float32, jnp.bfloat16
N = 512
BLOCKS = 8
CHUNKS = ((0, 1), (1, 1), (2, 1), (3, 1), (4, 1), (5, 1), (6, 1), (7, 1))
NCH = len(CHUNKS)
WIDEST = max(n for _, n in CHUNKS)
LAG = 4
OWN_FIRST = 0
AHEAD = 2
LOOK = 2
LAST = (((1,), (1,)), ((), ()))


def mod4(value):
    return lax.rem(value, 4)


def mix_matrix(mpo_ref, cmask_ref, bmask_ref, charge_ref, yh):
    rows = lax.broadcasted_iota(jnp.int32, (256, 16), 0)
    lane = lax.broadcasted_iota(jnp.int32, (256, 16), 1)
    want_v = lax.rem(rows // 16, 4) * 4 + yh
    pick_v = (lane == want_v).astype(F32)
    rows_s = lax.broadcasted_iota(jnp.int32, (256, 4), 0)
    lane_s = lax.broadcasted_iota(jnp.int32, (256, 4), 1)
    slots, _ = state_slots(charge_ref)
    pick_s = jnp.zeros((256, 4), F32)
    for s in range(4):
        hit = (lane_s == s) & (rows_s // 64 == slots[s])
        pick_s = jnp.where(hit, bmask_ref[s].astype(F32), pick_s)
    pick_s = pick_s.astype(BF16)
    cmask = cmask_ref[...].astype(F32).astype(BF16)
    allowed = lax.dot_general(pick_v.astype(BF16), cmask, LAST, preferred_element_type=F32)
    values = jnp.zeros((256, 16), F32)
    for w in range(16):
        coupling = jnp.dot(pick_s, mpo_ref[w], preferred_element_type=F32) * pick_v
        column = jnp.sum(coupling, axis=1, keepdims=True)
        values = jnp.where(lane == w, column, values)
    values = values * allowed
    spread_w = lax.broadcasted_iota(jnp.int32, (16, 256), 0)
    spread_c = lax.broadcasted_iota(jnp.int32, (16, 256), 1) // 16
    spread = (spread_w == lax.rem(spread_c, 4) * 4 + spread_c // 4).astype(BF16)
    full = jnp.dot(values.astype(BF16), spread, preferred_element_type=F32)
    row = lax.broadcasted_iota(jnp.int32, (256, 256), 0)
    col = lax.broadcasted_iota(jnp.int32, (256, 256), 1)
    return jnp.where(lax.rem(row, 16) == lax.rem(col, 16), full, 0.0).astype(BF16)


def state_slots(charge_ref):
    charge = [charge_ref[s] for s in range(4)]
    slots = []
    ones = jnp.int32(0)
    for s in range(4):
        slots.append(jnp.where(charge[s] == 1, 2 + ones, s - ones))
        ones = ones + charge[s]
    order = []
    for k in range(4):
        place = jnp.int32(0)
        for s in range(4):
            place = place + jnp.where(slots[s] == k, s, 0)
        order.append(place)
    return slots, order


def kernel(
    charge_in, bmask_in, env_ref, site_ref, mpo_in, cmask_in, psi_ref,
    new_env_ref, new_psi_ref,
    charge_ref, bmask_ref, mpo_ref, cmask_ref,
    site_v, srt, near, psi_v, psi_t, kmat, gath, mixed, sent, prod, turned, acc,
    other, half, wide, wide_in, summed, kept, ysend, yrecv,
    small_sem, site_sem, psi_sem, own_sem,
    x_send, x_recv, y_send, y_recv, r_send, r_recv, near_send, near_recv,
    p_send, p_recv, n_send, n_recv, z_send, z_recv, f_send, f_recv,
):
    g = lax.axis_index("section")
    c = lax.axis_index("channel")
    q = lax.axis_index("block")
    x, yh = c // 4, lax.rem(c, 4)
    up = lax.rem(q + 1, 16)
    down = lax.rem(q + 15, 16)
    target = jnp.where(g == 0, up, down)
    origin = jnp.where(g == 0, down, up)
    fed = jnp.where(g == 0, q > 0, q < 15)
    feeds = jnp.where(g == 0, q < 15, q > 0)
    at_x = [mod4(x + i) * 4 + yh for i in range(4)]
    at_y = [x * 4 + mod4(yh + i) for i in range(4)]
    spans = [pl.ds(first, count) for first, count in CHUNKS]

    def to(channel=None, block=None, section=None):
        where = {}
        if section is not None:
            where["section"] = section
        if channel is not None:
            where["channel"] = channel
        if block is not None:
            where["block"] = block
        return where

    def send(src, dst, send_sem, recv_sem, where):
        pltpu.make_async_remote_copy(
            src_ref=src, dst_ref=dst, send_sem=send_sem, recv_sem=recv_sem, device_id=where, device_id_type=MESH
        ).start()

    def took(ref, sem):
        pltpu.make_async_copy(ref, ref, sem).wait()

    small = [
        pltpu.make_async_copy(charge_in, charge_ref, small_sem.at[0]),
        pltpu.make_async_copy(bmask_in, bmask_ref, small_sem.at[1]),
        pltpu.make_async_copy(mpo_in, mpo_ref, small_sem.at[2]),
        pltpu.make_async_copy(cmask_in, cmask_ref, small_sem.at[3]),
    ]
    for copy in small:
        copy.start()
    own_in = pltpu.make_async_copy(env_ref.at[pl.ds(x * BLOCKS, BLOCKS)], gath.at[:, yh * 4 + x], own_sem)
    own_in.start()
    site_in = pltpu.make_async_copy(site_ref, site_v, site_sem)
    site_in.start()
    psi_in = pltpu.make_async_copy(psi_ref, psi_v, psi_sem)
    psi_in.start()

    barrier = pltpu.get_barrier_semaphore()
    for i in range(1, 4):
        pl.semaphore_signal(barrier, inc=1, device_id=to(channel=at_x[i]), device_id_type=MESH)
        pl.semaphore_signal(barrier, inc=1, device_id=to(channel=at_y[i]), device_id_type=MESH)
    pl.semaphore_signal(barrier, inc=1, device_id=to(section=1 - g), device_id_type=MESH)

    @pl.when(fed)
    def _():
        for i in range(4):
            pl.semaphore_signal(barrier, inc=1, device_id=to(channel=at_x[i], block=origin), device_id_type=MESH)

    pl.semaphore_wait(barrier, jnp.where(feeds, 11, 7))

    def pass_own(j):
        first, count = CHUNKS[j]
        mine = env_ref.at[pl.ds(x * BLOCKS + first, count)]
        there = gath.at[spans[j], yh * 4 + x]
        send(mine, there, y_send, y_recv.at[j, 0], to(channel=at_y[1]))
        send(mine, there, y_send, y_recv.at[j, 1], to(channel=at_y[3]))

    def swap(j):
        if j >= NCH:
            return
        first, count = CHUNKS[j]
        for i in range(1, 4):
            send(
                env_ref.at[pl.ds(mod4(x + i) * BLOCKS + first, count)], gath.at[spans[j], yh * 4 + x],
                x_send, x_recv.at[j], to(channel=at_x[i]),
            )
        if j < OWN_FIRST:
            pass_own(j)

    for j in range(AHEAD):
        swap(j)

    def pass_on(j):
        if j >= NCH:
            return
        took(gath.at[spans[j], pl.ds(0, 3)], x_recv.at[j])
        if j < OWN_FIRST:
            beside = x + 1 - 2 * lax.rem(x, 2)
            apart = 2 - 2 * (x // 2)
            parts = [gath.at[spans[j], pl.ds(yh * 4 + apart, 2)], gath.at[spans[j], yh * 4 + beside]]
        else:
            parts = [gath.at[spans[j], pl.ds(yh * 4, 4)]]
        for rows in parts:
            send(rows, rows, y_send, y_recv.at[j, 0], to(channel=at_y[1]))
            send(rows, rows, y_send, y_recv.at[j, 1], to(channel=at_y[3]))
        swap(j + AHEAD)

    def relay(j):
        four = gath.at[spans[j], pl.ds(0, 4)]
        before = gath.at[spans[j], pl.ds(mod4(yh + 3) * 4, 2)]
        took(four, y_recv.at[j, 0])
        send(before, before, r_send, r_recv.at[j, 0], to(channel=at_y[1]))
        after = gath.at[spans[j], pl.ds(mod4(yh + 1) * 4 + 2, 2)]
        took(four, y_recv.at[j, 1])
        send(after, after, r_send, r_recv.at[j, 1], to(channel=at_y[3]))

    def multiply(j):
        first, count = CHUNKS[j]
        for way in range(2):
            took(gath.at[spans[j], pl.ds(0, 2)], r_recv.at[j, way])
        for i in range(count):
            blended = jnp.dot(kmat[...], gath[first + i].reshape(256, N), preferred_element_type=F32)
            mixed[:, i] = blended.astype(BF16).reshape(4, 4, 16, N)
        for k in range(4):
            product = jnp.dot(mixed[k, 0:count].reshape(count * 64, N), srt[k], preferred_element_type=F32)
            product = product.astype(BF16).reshape(count, 4, 16, N)
            for vx in range(4):
                sent[first : first + count, vx * 4 + k] = product[:, vx]
        for i in range(1, 4):
            v = mod4(x + i)
            send(
                sent.at[spans[j], pl.ds(v * 4, 2)], prod.at[spans[j], pl.ds(x * 4, 2)],
                p_send, p_recv.at[j], to(channel=at_x[i]),
            )

        @pl.when(feeds)
        def _():
            for i in range(4):
                v = mod4(x + i)
                send(
                    sent.at[spans[j], pl.ds(v * 4 + 2, 2)], prod.at[spans[j], pl.ds(x * 4 + 2, 2)],
                    p_send, p_recv.at[j], to(channel=at_x[i], block=target),
                )

        prod[first : first + count, pl.ds(x * 4, 2)] = sent[first : first + count, pl.ds(x * 4, 2)]

    def turn(j):
        first, count = CHUNKS[j]
        for b in range(first, first + count):
            pieces = []
            for xs in range(4):
                rows = slice(xs * 128 + b * 16, xs * 128 + b * 16 + 16)
                pieces += [srt[0, rows, :], srt[1, rows, :], near[0, rows, :], near[1, rows, :]]
            turned[b] = jnp.concatenate(pieces, axis=0).T.reshape(4, 4, 32, 256)

    def gained(j, tile):
        first, count = CHUNKS[j]
        part = jnp.zeros((128, N), F32)
        for b in range(first, first + count):
            left = turned[(b, *tile)].reshape(128, 256)
            part = part + jnp.dot(left, prod[b].reshape(256, N), preferred_element_type=F32)
        return part.reshape(4, 32, N)

    def receive(j):
        @pl.when(fed)
        def _():
            took(prod.at[spans[j], pl.ds(0, 14)], p_recv.at[j])

        @pl.when(jnp.logical_not(fed))
        def _():
            took(prod.at[spans[j], pl.ds(0, 6)], p_recv.at[j])

    def accumulate(j):
        receive(j)

        def add(t, carry):
            part = gained(j, (t,))
            acc[t] = part if j == 0 else acc[t] + part
            return carry

        lax.fori_loop(0, 4, add, 0)

    def advance(tile, recv_sem):
        new_env_ref[tile] = (acc[tile] + gained(NCH - 1, tile)).astype(BF16)
        send(new_env_ref.at[tile], other.at[tile], n_send, recv_sem, to(section=1 - g))

    for copy in small:
        copy.wait()
    own_in.wait()
    pass_on(0)
    site_in.wait()
    _, order = state_slots(charge_ref)
    for k in (2, 3, 0, 1):
        srt[k] = site_v[order[k]]
        if k == 3:

            @pl.when(feeds)
            def _():
                send(srt.at[pl.ds(2, 2)], near, near_send, near_recv, to(block=target))

    for j in range(1, LOOK):
        pass_on(j)
    kmat[...] = mix_matrix(mpo_ref, cmask_ref, bmask_ref, charge_ref, yh)

    for j in range(NCH):
        relay(j)
        pass_on(j + LOOK)
        if j == 1:
            psi_in.wait()

            @pl.when(g == 0)
            def _():
                psi_t[...] = psi_v[...]

            @pl.when(g == 1)
            def _():
                psi_t[...] = psi_v[...].T

        if j == LAG - 1:
            @pl.when(fed)
            def _():
                took(near, near_recv)

            @pl.when(jnp.logical_not(fed))
            def _():
                near[...] = jnp.zeros_like(near)
                for xs in range(4):
                    prod[:, xs * 4 + 2 : xs * 4 + 4] = jnp.zeros((BLOCKS, 2, 16, N), BF16)

        if j >= LAG:
            accumulate(j - LAG)
        if j >= 1:
            multiply(j - 1)
        for b in (2 * (j - LAG + 1), 2 * (j - LAG + 1) + 1):
            if 0 <= b < NCH:
                turn(b)
    accumulate(NCH - LAG)
    multiply(NCH - 1)
    for j in range(NCH - LAG + 1, NCH - 1):
        accumulate(j)

    receive(NCH - 1)
    all_rows = slice(None)
    hand = [mod4(yh + d) for d in range(4)]

    @pl.when(g == 0)
    def _():
        for d in (1, 2, 3, 0):
            advance((all_rows, hand[d]), n_recv.at[d])

    @pl.when(g == 1)
    def _():
        for t in range(4):
            advance((t,), n_recv.at[t])

    for t in range(4):
        rows = new_env_ref[t].reshape(128, N)
        half[t] = jnp.dot(rows, psi_t[...], preferred_element_type=F32).astype(BF16).reshape(4, 32, N)
    quarter = other.at[0]

    @pl.when(g == 0)
    def _():
        def settle(t):
            columns = slice(t * 128, t * 128 + 128)
            took(wide_in.at[pl.ds(0, 3), :, :, columns], z_recv.at[t])
            total = wide[x, :, :, columns].astype(F32)
            for d in range(1, 4):
                total = total + wide_in[mod4(x + d), :, :, columns].astype(F32)
            summed[:, :, columns] = total
            ysend[:, :, columns] = total.astype(BF16)
            for d in range(1, 4):
                send(
                    ysend.at[hand[d], :, columns], yrecv.at[yh, :, columns],
                    f_send, f_recv, to(channel=at_y[d]),
                )

        for t in range(4):
            columns = slice(t * 128, t * 128 + 128)
            took(quarter, n_recv.at[t])
            part = lax.dot_general(half[...].reshape(N, N), other[t].reshape(128, N), LAST, preferred_element_type=F32)
            wide[:, :, :, columns] = part.astype(BF16).reshape(4, 4, 32, 128)
            for d in range(1, 4):
                send(
                    wide.at[mod4(x + d), :, :, columns], wide_in.at[x, :, :, columns],
                    z_send, z_recv.at[t], to(channel=at_x[d]),
                )
            if t:
                settle(t - 1)
        settle(3)
        kept[...] = summed[yh]

    @pl.when(g == 1)
    def _():
        def settle(d):
            took(wide_in.at[d, pl.ds(0, 3)], z_recv.at[d])
            total = wide[d, x].astype(F32)
            for e in range(1, 4):
                total = total + wide_in[d, mod4(x + e)].astype(F32)
            if d:
                ysend[d] = total.astype(BF16)
                send(ysend.at[d], yrecv.at[yh], f_send, f_recv, to(channel=at_y[d]))
            else:
                kept[...] = total

        for d in (1, 2, 3, 0):
            took(quarter, n_recv.at[d])
            rows = other[:, hand[d]].reshape(128, N)
            part = lax.dot_general(rows, half[...].reshape(N, N), LAST, preferred_element_type=F32)
            wide[d] = part.astype(BF16).reshape(4, 32, N)
            for e in range(1, 4):
                send(wide.at[d, mod4(x + e)], wide_in.at[d, x], z_send, z_recv.at[d], to(channel=at_x[e]))
            if d != 1:
                settle((d + 3) % 4)
        settle(0)

    took(gath.at[:, 0:3], x_send)
    took(gath.at[:, 0:8], y_send)
    took(gath.at[:, 0:4], r_send)

    @pl.when(feeds)
    def _():
        took(near, near_send)
        took(sent.at[:, 0:14], p_send)

    @pl.when(jnp.logical_not(feeds))
    def _():
        took(sent.at[:, 0:6], p_send)

    took(new_env_ref, n_send)
    took(wide_in.at[pl.ds(0, 3)], z_send)
    took(yrecv.at[pl.ds(0, 3)], f_recv)
    result = kept[...]
    for d in range(1, 4):
        result = result + yrecv[mod4(yh + d)].astype(F32)
    new_psi_ref[...] = result.astype(BF16)
    took(ysend.at[pl.ds(0, 3)], f_send)


def per_device(env, site_tensor, mpo, channel_mask, block_mask, state_charge, psi):
    dma = pltpu.SemaphoreType.DMA
    hbm = pl.BlockSpec(memory_space=pltpu.HBM)
    vmem = pl.BlockSpec(memory_space=pltpu.VMEM)
    new_env, new_psi = pl.pallas_call(
        kernel,
        out_shape=(pltpu.VMEM((4, 4, 32, N), BF16), pltpu.VMEM((32, N), BF16)),
        in_specs=[hbm] * 7,
        out_specs=(vmem, vmem),
        scratch_shapes=[
            pltpu.SMEM((4,), jnp.int32),
            pltpu.SMEM((4,), jnp.int32),
            pltpu.VMEM((16, 4, 16), BF16),
            pltpu.VMEM((16, 16), jnp.int32),
            pltpu.VMEM((4, N, N), BF16),
            pltpu.VMEM((4, N, N), BF16),
            pltpu.VMEM((2, N, N), BF16),
            pltpu.VMEM((N, N), BF16),
            pltpu.VMEM((N, N), BF16),
            pltpu.VMEM((256, 256), BF16),
            pltpu.VMEM((BLOCKS, 16, 16, N), BF16),
            pltpu.VMEM((4, WIDEST, 4, 16, N), BF16),
            pltpu.VMEM((BLOCKS, 16, 16, N), BF16),
            pltpu.VMEM((BLOCKS, 16, 16, N), BF16),
            pltpu.VMEM((BLOCKS, 4, 4, 32, 256), BF16),
            pltpu.VMEM((4, 4, 32, N), F32),
            pltpu.VMEM((4, 4, 32, N), BF16),
            pltpu.VMEM((4, 4, 32, N), BF16),
            pltpu.VMEM((4, 4, 32, N), BF16),
            pltpu.VMEM((4, 4, 32, N), BF16),
            pltpu.VMEM((4, 32, N), F32),
            pltpu.VMEM((32, N), F32),
            pltpu.VMEM((4, 32, N), BF16),
            pltpu.VMEM((4, 32, N), BF16),
            dma((4,)), dma, dma, dma,
            dma, dma((NCH,)), dma, dma((NCH, 2)), dma, dma((NCH, 2)), dma, dma,
            dma, dma((NCH,)), dma, dma((4,)), dma, dma((4,)), dma, dma,
        ],
        compiler_params=pltpu.CompilerParams(
            collective_id=0, has_side_effects=True, vmem_limit_bytes=56 * 1024 * 1024
        ),
    )(
        *[
            pltpu.with_memory_space_constraint(a, pltpu.HBM)
            for a in (
                state_charge,
                block_mask.reshape(4),
                env.reshape(4 * BLOCKS, 16, N),
                site_tensor.reshape(4, N, N),
                jnp.swapaxes(mpo[0], 1, 2),
                channel_mask[0],
                psi.reshape(N, N),
            )
        ]
    )
    return new_env.reshape(1, 1, 1, N, N), new_psi.reshape(32, 1, 1, N)


def solution(mesh):
    return jax.shard_map(
        per_device,
        mesh=mesh,
        in_specs=(
            P("section", "channel", "block", None, None),
            P("section", None, "block", None, None),
            P("section", None, None, None),
            P("section", None, None),
            P("section", None, "block"),
            P(),
            P("section", "block", None, None),
        ),
        out_specs=(
            P("section", "channel", "block", None, None),
            P("channel", "section", "block", None),
        ),
        check_vma=False,
    )
```

```python
import functools

import jax
import jax.numpy as jnp
from jax import lax
from jax.experimental import pallas as pl
from jax.experimental.pallas import tpu as pltpu
from jax.sharding import PartitionSpec as P

MESH = pl.DeviceIdType.MESH
F32, BF16 = jnp.float32, jnp.bfloat16
N = 512
BLOCKS = 8
CHUNKS = ((0, 1), (1, 1), (2, 1), (3, 1), (4, 1), (5, 1), (6, 1), (7, 1))
NCH = len(CHUNKS)
WIDEST = max(n for _, n in CHUNKS)
LAG = 4
OWN_FIRST = 0
AHEAD = 2
LOOK = 2
LAST = (((1,), (1,)), ((), ()))


def mod4(value):
    return lax.rem(value, 4)


def mix_matrix(mpo_ref, cmask_ref, bmask_ref, charge_ref, yh):
    rows = lax.broadcasted_iota(jnp.int32, (256, 16), 0)
    lane = lax.broadcasted_iota(jnp.int32, (256, 16), 1)
    want_v = lax.rem(rows // 16, 4) * 4 + yh
    pick_v = (lane == want_v).astype(F32)
    rows_s = lax.broadcasted_iota(jnp.int32, (256, 4), 0)
    lane_s = lax.broadcasted_iota(jnp.int32, (256, 4), 1)
    slots, _ = state_slots(charge_ref)
    pick_s = jnp.zeros((256, 4), F32)
    for s in range(4):
        hit = (lane_s == s) & (rows_s // 64 == slots[s])
        pick_s = jnp.where(hit, bmask_ref[s].astype(F32), pick_s)
    pick_s = pick_s.astype(BF16)
    cmask = cmask_ref[...].astype(F32).astype(BF16)
    allowed = lax.dot_general(pick_v.astype(BF16), cmask, LAST, preferred_element_type=F32)
    values = jnp.zeros((256, 16), F32)
    for w in range(16):
        coupling = jnp.dot(pick_s, mpo_ref[w], preferred_element_type=F32) * pick_v
        column = jnp.sum(coupling, axis=1, keepdims=True)
        values = jnp.where(lane == w, column, values)
    values = values * allowed
    spread_w = lax.broadcasted_iota(jnp.int32, (16, 256), 0)
    spread_c = lax.broadcasted_iota(jnp.int32, (16, 256), 1) // 16
    spread = (spread_w == lax.rem(spread_c, 4) * 4 + spread_c // 4).astype(BF16)
    full = jnp.dot(values.astype(BF16), spread, preferred_element_type=F32)
    row = lax.broadcasted_iota(jnp.int32, (256, 256), 0)
    col = lax.broadcasted_iota(jnp.int32, (256, 256), 1)
    return jnp.where(lax.rem(row, 16) == lax.rem(col, 16), full, 0.0).astype(BF16)


def state_slots(charge_ref):
    charge = [charge_ref[s] for s in range(4)]
    slots = []
    ones = jnp.int32(0)
    for s in range(4):
        slots.append(jnp.where(charge[s] == 1, 2 + ones, s - ones))
        ones = ones + charge[s]
    order = []
    for k in range(4):
        place = jnp.int32(0)
        for s in range(4):
            place = place + jnp.where(slots[s] == k, s, 0)
        order.append(place)
    return slots, order


def kernel(
    charge_in, bmask_in, env_ref, site_ref, mpo_in, cmask_in, psi_ref,
    new_env_ref, new_psi_ref,
    charge_ref, bmask_ref, mpo_ref, cmask_ref,
    site_v, srt, near, psi_v, psi_t, kmat, gath, mixed, sent, prod, turned, acc,
    other, half, wide, wide_in, summed, kept, ysend, yrecv,
    small_sem, site_sem, psi_sem, own_sem,
    x_send, x_recv, y_send, y_recv, r_send, r_recv, near_send, near_recv,
    p_send, p_recv, n_send, n_recv, z_send, z_recv, f_send, f_recv,
):
    g = lax.axis_index("section")
    c = lax.axis_index("channel")
    q = lax.axis_index("block")
    x, yh = c // 4, lax.rem(c, 4)
    up = lax.rem(q + 1, 16)
    down = lax.rem(q + 15, 16)
    target = jnp.where(g == 0, up, down)
    origin = jnp.where(g == 0, down, up)
    fed = jnp.where(g == 0, q > 0, q < 15)
    feeds = jnp.where(g == 0, q < 15, q > 0)
    at_x = [mod4(x + i) * 4 + yh for i in range(4)]
    at_y = [x * 4 + mod4(yh + i) for i in range(4)]
    spans = [pl.ds(first, count) for first, count in CHUNKS]

    def to(channel=None, block=None, section=None):
        where = {}
        if section is not None:
            where["section"] = section
        if channel is not None:
            where["channel"] = channel
        if block is not None:
            where["block"] = block
        return where

    def send(src, dst, send_sem, recv_sem, where):
        pltpu.make_async_remote_copy(
            src_ref=src, dst_ref=dst, send_sem=send_sem, recv_sem=recv_sem, device_id=where, device_id_type=MESH
        ).start()

    def took(ref, sem):
        pltpu.make_async_copy(ref, ref, sem).wait()

    small = [
        pltpu.make_async_copy(charge_in, charge_ref, small_sem.at[0]),
        pltpu.make_async_copy(bmask_in, bmask_ref, small_sem.at[1]),
        pltpu.make_async_copy(mpo_in, mpo_ref, small_sem.at[2]),
        pltpu.make_async_copy(cmask_in, cmask_ref, small_sem.at[3]),
    ]
    for copy in small:
        copy.start()
    own_in = pltpu.make_async_copy(env_ref.at[pl.ds(x * BLOCKS, BLOCKS)], gath.at[:, yh * 4 + x], own_sem)
    own_in.start()
    site_in = pltpu.make_async_copy(site_ref, site_v, site_sem)
    site_in.start()
    psi_in = pltpu.make_async_copy(psi_ref, psi_v, psi_sem)
    psi_in.start()

    barrier = pltpu.get_barrier_semaphore()
    for i in range(1, 4):
        pl.semaphore_signal(barrier, inc=1, device_id=to(channel=at_x[i]), device_id_type=MESH)
        pl.semaphore_signal(barrier, inc=1, device_id=to(channel=at_y[i]), device_id_type=MESH)
    pl.semaphore_signal(barrier, inc=1, device_id=to(section=1 - g), device_id_type=MESH)

    @pl.when(fed)
    def _():
        for i in range(4):
            pl.semaphore_signal(barrier, inc=1, device_id=to(channel=at_x[i], block=origin), device_id_type=MESH)

    pl.semaphore_wait(barrier, jnp.where(feeds, 11, 7))

    def pass_own(j):
        first, count = CHUNKS[j]
        mine = env_ref.at[pl.ds(x * BLOCKS + first, count)]
        there = gath.at[spans[j], yh * 4 + x]
        send(mine, there, y_send, y_recv.at[j, 0], to(channel=at_y[1]))
        send(mine, there, y_send, y_recv.at[j, 1], to(channel=at_y[3]))

    def swap(j):
        if j >= NCH:
            return
        first, count = CHUNKS[j]
        for i in range(1, 4):
            send(
                env_ref.at[pl.ds(mod4(x + i) * BLOCKS + first, count)], gath.at[spans[j], yh * 4 + x],
                x_send, x_recv.at[j], to(channel=at_x[i]),
            )
        if j < OWN_FIRST:
            pass_own(j)

    for j in range(AHEAD):
        swap(j)

    def pass_on(j):
        if j >= NCH:
            return
        took(gath.at[spans[j], pl.ds(0, 3)], x_recv.at[j])
        if j < OWN_FIRST:
            beside = x + 1 - 2 * lax.rem(x, 2)
            apart = 2 - 2 * (x // 2)
            parts = [gath.at[spans[j], pl.ds(yh * 4 + apart, 2)], gath.at[spans[j], yh * 4 + beside]]
        else:
            parts = [gath.at[spans[j], pl.ds(yh * 4, 4)]]
        for rows in parts:
            send(rows, rows, y_send, y_recv.at[j, 0], to(channel=at_y[1]))
            send(rows, rows, y_send, y_recv.at[j, 1], to(channel=at_y[3]))
        swap(j + AHEAD)

    def relay(j):
        four = gath.at[spans[j], pl.ds(0, 4)]
        before = gath.at[spans[j], pl.ds(mod4(yh + 3) * 4, 2)]
        took(four, y_recv.at[j, 0])
        send(before, before, r_send, r_recv.at[j, 0], to(channel=at_y[1]))
        after = gath.at[spans[j], pl.ds(mod4(yh + 1) * 4 + 2, 2)]
        took(four, y_recv.at[j, 1])
        send(after, after, r_send, r_recv.at[j, 1], to(channel=at_y[3]))

    def multiply(j):
        first, count = CHUNKS[j]
        for way in range(2):
            took(gath.at[spans[j], pl.ds(0, 2)], r_recv.at[j, way])
        for i in range(count):
            blended = jnp.dot(kmat[...], gath[first + i].reshape(256, N), preferred_element_type=F32)
            mixed[:, i] = blended.astype(BF16).reshape(4, 4, 16, N)
        for k in range(4):
            product = jnp.dot(mixed[k, 0:count].reshape(count * 64, N), srt[k], preferred_element_type=F32)
            product = product.astype(BF16).reshape(count, 4, 16, N)
            for vx in range(4):
                sent[first : first + count, vx * 4 + k] = product[:, vx]
        for i in (2, 1, 3):
            v = mod4(x + i)
            send(
                sent.at[spans[j], pl.ds(v * 4, 2)], prod.at[spans[j], pl.ds(x * 4, 2)],
                p_send, p_recv.at[j], to(channel=at_x[i]),
            )

        @pl.when(feeds)
        def _():
            for i in (2, 1, 3, 0):
                v = mod4(x + i)
                send(
                    sent.at[spans[j], pl.ds(v * 4 + 2, 2)], prod.at[spans[j], pl.ds(x * 4 + 2, 2)],
                    p_send, p_recv.at[j], to(channel=at_x[i], block=target),
                )

        prod[first : first + count, pl.ds(x * 4, 2)] = sent[first : first + count, pl.ds(x * 4, 2)]

    def turn(j):
        first, count = CHUNKS[j]
        for b in range(first, first + count):
            pieces = []
            for xs in range(4):
                rows = slice(xs * 128 + b * 16, xs * 128 + b * 16 + 16)
                pieces += [srt[0, rows, :], srt[1, rows, :], near[0, rows, :], near[1, rows, :]]
            turned[b] = jnp.concatenate(pieces, axis=0).T.reshape(4, 4, 32, 256)

    def gained(j, tile):
        first, count = CHUNKS[j]
        part = jnp.zeros((128, N), F32)
        for b in range(first, first + count):
            left = turned[(b, *tile)].reshape(128, 256)
            part = part + jnp.dot(left, prod[b].reshape(256, N), preferred_element_type=F32)
        return part.reshape(4, 32, N)

    def receive(j):
        @pl.when(fed)
        def _():
            took(prod.at[spans[j], pl.ds(0, 14)], p_recv.at[j])

        @pl.when(jnp.logical_not(fed))
        def _():
            took(prod.at[spans[j], pl.ds(0, 6)], p_recv.at[j])

    def accumulate(j):
        receive(j)

        def add(t, carry):
            part = gained(j, (t,))
            acc[t] = part if j == 0 else acc[t] + part
            return carry

        lax.fori_loop(0, 4, add, 0)

    def advance(tile, recv_sem):
        new_env_ref[tile] = (acc[tile] + gained(NCH - 1, tile)).astype(BF16)
        send(new_env_ref.at[tile], other.at[tile], n_send, recv_sem, to(section=1 - g))

    for copy in small:
        copy.wait()
    own_in.wait()
    pass_on(0)
    site_in.wait()
    _, order = state_slots(charge_ref)
    for k in (2, 3, 0, 1):
        srt[k] = site_v[order[k]]
        if k == 3:

            @pl.when(feeds)
            def _():
                send(srt.at[pl.ds(2, 2)], near, near_send, near_recv, to(block=target))

    for j in range(1, LOOK):
        pass_on(j)
    kmat[...] = mix_matrix(mpo_ref, cmask_ref, bmask_ref, charge_ref, yh)

    for j in range(NCH):
        relay(j)
        pass_on(j + LOOK)
        if j == 1:
            psi_in.wait()

            @pl.when(g == 0)
            def _():
                psi_t[...] = psi_v[...]

            @pl.when(g == 1)
            def _():
                psi_t[...] = psi_v[...].T

        if j == LAG - 1:
            @pl.when(fed)
            def _():
                took(near, near_recv)

            @pl.when(jnp.logical_not(fed))
            def _():
                near[...] = jnp.zeros_like(near)
                for xs in range(4):
                    prod[:, xs * 4 + 2 : xs * 4 + 4] = jnp.zeros((BLOCKS, 2, 16, N), BF16)

        if j >= LAG:
            accumulate(j - LAG)
        if j >= 1:
            multiply(j - 1)
        for b in (2 * (j - LAG + 1), 2 * (j - LAG + 1) + 1):
            if 0 <= b < NCH:
                turn(b)
    accumulate(NCH - LAG)
    multiply(NCH - 1)
    for j in range(NCH - LAG + 1, NCH - 1):
        accumulate(j)

    receive(NCH - 1)
    all_rows = slice(None)
    hand = [mod4(yh + d) for d in range(4)]

    @pl.when(g == 0)
    def _():
        for d in (1, 2, 3, 0):
            advance((all_rows, hand[d]), n_recv.at[d])

    @pl.when(g == 1)
    def _():
        for t in range(4):
            advance((t,), n_recv.at[t])

    for t in range(4):
        rows = new_env_ref[t].reshape(128, N)
        half[t] = jnp.dot(rows, psi_t[...], preferred_element_type=F32).astype(BF16).reshape(4, 32, N)
    quarter = other.at[0]

    @pl.when(g == 0)
    def _():
        def settle(t):
            columns = slice(t * 128, t * 128 + 128)
            took(wide_in.at[pl.ds(0, 3), :, :, columns], z_recv.at[t])
            total = wide[x, :, :, columns].astype(F32)
            for d in range(1, 4):
                total = total + wide_in[mod4(x + d), :, :, columns].astype(F32)
            summed[:, :, columns] = total
            ysend[:, :, columns] = total.astype(BF16)
            for d in range(1, 4):
                send(
                    ysend.at[hand[d], :, columns], yrecv.at[yh, :, columns],
                    f_send, f_recv, to(channel=at_y[d]),
                )

        for t in range(4):
            columns = slice(t * 128, t * 128 + 128)
            took(quarter, n_recv.at[t])
            part = lax.dot_general(half[...].reshape(N, N), other[t].reshape(128, N), LAST, preferred_element_type=F32)
            wide[:, :, :, columns] = part.astype(BF16).reshape(4, 4, 32, 128)
            for d in range(1, 4):
                send(
                    wide.at[mod4(x + d), :, :, columns], wide_in.at[x, :, :, columns],
                    z_send, z_recv.at[t], to(channel=at_x[d]),
                )
            if t:
                settle(t - 1)
        settle(3)
        kept[...] = summed[yh]

    @pl.when(g == 1)
    def _():
        def settle(d):
            took(wide_in.at[d, pl.ds(0, 3)], z_recv.at[d])
            total = wide[d, x].astype(F32)
            for e in range(1, 4):
                total = total + wide_in[d, mod4(x + e)].astype(F32)
            if d:
                ysend[d] = total.astype(BF16)
                send(ysend.at[d], yrecv.at[yh], f_send, f_recv, to(channel=at_y[d]))
            else:
                kept[...] = total

        for d in (1, 2, 3, 0):
            took(quarter, n_recv.at[d])
            rows = other[:, hand[d]].reshape(128, N)
            part = lax.dot_general(rows, half[...].reshape(N, N), LAST, preferred_element_type=F32)
            wide[d] = part.astype(BF16).reshape(4, 32, N)
            for e in range(1, 4):
                send(wide.at[d, mod4(x + e)], wide_in.at[d, x], z_send, z_recv.at[d], to(channel=at_x[e]))
            if d != 1:
                settle((d + 3) % 4)
        settle(0)

    took(gath.at[:, 0:3], x_send)
    took(gath.at[:, 0:8], y_send)
    took(gath.at[:, 0:4], r_send)

    @pl.when(feeds)
    def _():
        took(near, near_send)
        took(sent.at[:, 0:14], p_send)

    @pl.when(jnp.logical_not(feeds))
    def _():
        took(sent.at[:, 0:6], p_send)

    took(new_env_ref, n_send)
    took(wide_in.at[pl.ds(0, 3)], z_send)
    took(yrecv.at[pl.ds(0, 3)], f_recv)
    result = kept[...]
    for d in range(1, 4):
        result = result + yrecv[mod4(yh + d)].astype(F32)
    new_psi_ref[...] = result.astype(BF16)
    took(ysend.at[pl.ds(0, 3)], f_send)


def per_device(env, site_tensor, mpo, channel_mask, block_mask, state_charge, psi):
    dma = pltpu.SemaphoreType.DMA
    hbm = pl.BlockSpec(memory_space=pltpu.HBM)
    vmem = pl.BlockSpec(memory_space=pltpu.VMEM)
    new_env, new_psi = pl.pallas_call(
        kernel,
        out_shape=(pltpu.VMEM((4, 4, 32, N), BF16), pltpu.VMEM((32, N), BF16)),
        in_specs=[hbm] * 7,
        out_specs=(vmem, vmem),
        scratch_shapes=[
            pltpu.SMEM((4,), jnp.int32),
            pltpu.SMEM((4,), jnp.int32),
            pltpu.VMEM((16, 4, 16), BF16),
            pltpu.VMEM((16, 16), jnp.int32),
            pltpu.VMEM((4, N, N), BF16),
            pltpu.VMEM((4, N, N), BF16),
            pltpu.VMEM((2, N, N), BF16),
            pltpu.VMEM((N, N), BF16),
            pltpu.VMEM((N, N), BF16),
            pltpu.VMEM((256, 256), BF16),
            pltpu.VMEM((BLOCKS, 16, 16, N), BF16),
            pltpu.VMEM((4, WIDEST, 4, 16, N), BF16),
            pltpu.VMEM((BLOCKS, 16, 16, N), BF16),
            pltpu.VMEM((BLOCKS, 16, 16, N), BF16),
            pltpu.VMEM((BLOCKS, 4, 4, 32, 256), BF16),
            pltpu.VMEM((4, 4, 32, N), F32),
            pltpu.VMEM((4, 4, 32, N), BF16),
            pltpu.VMEM((4, 4, 32, N), BF16),
            pltpu.VMEM((4, 4, 32, N), BF16),
            pltpu.VMEM((4, 4, 32, N), BF16),
            pltpu.VMEM((4, 32, N), F32),
            pltpu.VMEM((32, N), F32),
            pltpu.VMEM((4, 32, N), BF16),
            pltpu.VMEM((4, 32, N), BF16),
            dma((4,)), dma, dma, dma,
            dma, dma((NCH,)), dma, dma((NCH, 2)), dma, dma((NCH, 2)), dma, dma,
            dma, dma((NCH,)), dma, dma((4,)), dma, dma((4,)), dma, dma,
        ],
        compiler_params=pltpu.CompilerParams(
            collective_id=0, has_side_effects=True, vmem_limit_bytes=56 * 1024 * 1024
        ),
    )(
        *[
            pltpu.with_memory_space_constraint(a, pltpu.HBM)
            for a in (
                state_charge,
                block_mask.reshape(4),
                env.reshape(4 * BLOCKS, 16, N),
                site_tensor.reshape(4, N, N),
                jnp.swapaxes(mpo[0], 1, 2),
                channel_mask[0],
                psi.reshape(N, N),
            )
        ]
    )
    return new_env.reshape(1, 1, 1, N, N), new_psi.reshape(32, 1, 1, N)


def solution(mesh):
    return jax.shard_map(
        per_device,
        mesh=mesh,
        in_specs=(
            P("section", "channel", "block", None, None),
            P("section", None, "block", None, None),
            P("section", None, None, None),
            P("section", None, None),
            P("section", None, "block"),
            P(),
            P("section", "block", None, None),
        ),
        out_specs=(
            P("section", "channel", "block", None, None),
            P("channel", "section", "block", None),
        ),
        check_vma=False,
    )
```
